32 devices in a mesh: basin: 8 (over y, x, core), tile: 4 (over z).
Axes of the slice: x: 2, y: 2, z: 4, core: 2. Of those that a mesh axis runs over, the one named last changes fastest.
Arguments:
- tile_water: float32 [8, 64, 4096], P('basin', None, 'tile'), may hold values from 0.1 to 3
- tile_frac: float32 [8, 64, 4096], P('basin', None, 'tile'), may hold values from 0.01 to 0.12
- tile_cell: int32 [8, 64, 4096], P('basin', None, 'tile'), may hold values from 0 to 255
- storage: float32 [8, 64, 256], P('basin', 'tile'), may hold values from 0 to 2
- kappa: float32 [8, 64, 256], P('basin', 'tile'), may hold values from 0.4 to 1
- inverse: float32 [8, 64, 256, 256], P('basin', 'tile'), may hold values from -0.25 to 1.15
- cell_mask: int32 [8, 64, 256], P('basin', 'tile'), may hold values 0 or 1
- upstream: int32 [8, 64], P('basin', 'tile'), may hold values from 0 to 15, as said below
Outputs:
- level: float32 [8, 64, 256], P('basin', 'tile')
- discharge: float32 [8, 64, 256], P('basin', 'tile')
The draws below stay inside these ranges and needn't reach their ends.
Inputs may be any that keep to these rules, and one draw needn't show every extreme that they name: `upstream`: for each reach position and each group of 16 consecutive chains, the values form a permutation of 0 to 15.
All inputs are finite; a program needn't handle non-finite values. No bound on the sum of `cell_mask` on one device may be relied on, other than what follows from the above.
Results may differ from the reference program's by a relative error of at most 0.0001.
Values sent between devices are 32-bit elements; how exact they have to be, the bound alone decides.
A program may use at most 64 MiB of HBM per device.

```python
import math
import jax
import jax.numpy as jnp
from jax import lax

BLOCK = 256
CH_DEV = 16
SUBSTEPS = 3
CHAINS = 64
POSITIONS = 8
TPB = 4096


def draw_inverse(key, part):
    shape = (POSITIONS, CHAINS, BLOCK, BLOCK)
    noise = jnp.clip(jax.random.normal(key, shape, jnp.float32), -4.0, 4.0) * (0.3 / BLOCK ** 0.5)
    return noise + 0.9 * jnp.eye(BLOCK, dtype=jnp.float32)


def draw_upstream(key, part):
    keys = jax.random.split(jax.random.fold_in(key, 7), POSITIONS * (CHAINS // CH_DEV))
    perms = jax.vmap(lambda single: jax.random.permutation(single, CH_DEV))(keys)
    return perms.reshape(POSITIONS, CHAINS).astype(jnp.int32)


def plant(values, stream_key, least, high):
    longest = values.shape.index(max(values.shape))
    spots = []
    for shift in (0, 1):
        where = [jax.random.randint(jax.random.fold_in(stream_key, axis), (), 0, length) for axis, length in enumerate(values.shape)]
        where[longest] = (where[longest] + shift) % values.shape[longest]
        spots.append(tuple(where))
    return values.at[spots[0]].set(least).at[spots[1]].set(high)


def shard_levels(stream_key, extent, shards, least, largest):
    def one(axis_at, shards_of):
        steps = jax.random.uniform(jax.random.fold_in(jax.random.fold_in(stream_key, 6), axis_at), (shards_of,), jnp.float32, least / len(shards), largest / len(shards))
        return jnp.repeat(jnp.exp(steps), extent[axis_at] // shards_of).reshape((-1,) + (1,) * (len(extent) - axis_at - 1))

    level = one(*shards[0])
    for cut in shards[1:]:
        level = level * one(*cut)
    return level


def setup_inputs(seed: int = 0) -> dict:
    streams_of = jax.random.split(jax.random.key(seed), 9)
    return {
        "tile_water": jnp.clip(jnp.exp(math.log(3.0) - 3.4011974 * jax.random.uniform(streams_of[0], (POSITIONS, CHAINS, TPB), jnp.float32) ** shard_levels(streams_of[0], (POSITIONS, CHAINS, TPB), ((0, 8), (2, 4)), -0.2, 0.2)), 0.1, 3.0),
        "tile_frac": jnp.clip(jnp.exp(math.log(0.12) - 2.4849066 * jax.random.uniform(streams_of[1], (POSITIONS, CHAINS, TPB), jnp.float32) ** shard_levels(streams_of[1], (POSITIONS, CHAINS, TPB), ((0, 8), (2, 4)), -0.2, 0.2)), 0.01, 0.12),
        "tile_cell": plant(jax.random.randint(streams_of[2], (POSITIONS, CHAINS, TPB), 0, BLOCK), jax.random.fold_in(streams_of[2], 1), 0, BLOCK - 1).astype(jnp.int32),
        "storage": jnp.clip(2.0 * jax.random.uniform(streams_of[3], (POSITIONS, CHAINS, BLOCK), jnp.float32) ** shard_levels(streams_of[3], (POSITIONS, CHAINS, BLOCK), ((0, 8), (1, 4)), -0.2, 0.2), 0.0, 2.0),
        "kappa": jnp.clip(0.4 + 0.6 * jax.random.uniform(streams_of[4], (POSITIONS, CHAINS, BLOCK), jnp.float32) ** shard_levels(streams_of[4], (POSITIONS, CHAINS, BLOCK), ((0, 8), (1, 4)), -0.2, 0.2), 0.4, 1.0),
        "inverse": draw_inverse(jax.random.fold_in(streams_of[8], 71), 0),
        "cell_mask": plant((jax.random.randint(streams_of[6], (POSITIONS, CHAINS, BLOCK), 0, 8) < 7).astype(jnp.int32), jax.random.fold_in(streams_of[6], 1), 0, 1),
        "upstream": draw_upstream(jax.random.fold_in(streams_of[8], 71), 0),
    }


time_step = 0.5


def reference(tile_water, tile_frac, tile_cell, storage, kappa, inverse, cell_mask, upstream):
    npos, chains, width = storage.shape
    blocks = jnp.arange(npos * chains, dtype=jnp.int32).reshape(npos, chains, 1)
    ids = (blocks * width + tile_cell).reshape(-1)
    runoff = jax.ops.segment_sum((tile_frac * tile_water).reshape(-1), ids, num_segments=npos * chains * width)
    forcing = time_step * runoff.reshape(npos, chains, width)
    mask = cell_mask.astype(jnp.float32)
    groups = (jnp.arange(chains, dtype=jnp.int32) // CH_DEV) * CH_DEV
    sources = upstream + groups[None, :]
    level = storage
    discharge = storage
    for substep in range(SUBSTEPS):
        def advance(previous, items):
            lev, force, msk, rate, matrix, src = items
            inflow = jnp.take(previous, src, axis=0)
            vector = lev + force + inflow
            wet = msk * jnp.einsum("cjk,ck->cj", matrix, vector, precision=lax.Precision.HIGHEST)
            outflow = rate * wet
            return outflow, (wet - outflow, outflow)
        start = jnp.zeros((chains, width), jnp.float32)
        _, (level, discharge) = lax.scan(advance, start, (level, forcing, mask, kappa, inverse, sources))
    return level, discharge
```

```python
import functools

import jax
import jax.numpy as jnp
from jax import lax
from jax.experimental import pallas as pl
from jax.experimental.pallas import tpu as pltpu
from jax.sharding import PartitionSpec as P

SUBSTEPS = 3
time_step = 0.5
MESH = pl.DeviceIdType.MESH
NT = (((1,), (1,)), ((), ()))


def two_terms(value):
    head = value.astype(jnp.bfloat16)
    return head, (value - head.astype(jnp.float32)).astype(jnp.bfloat16)


def iota(shape, axis):
    return lax.broadcasted_iota(jnp.int32, shape, axis)


def kernel(npos, nset, water_hbm, frac_hbm, cell_hbm, storage_ref, kappa_ref, inverse_hbm, mask_ref, upstream_ref,
           level_ref, discharge_ref,
           water, frac, cell, inverse, heads, tails, part, arrived, flow, inflow,
           tile_sem, inverse_sem, part_send, part_recv, flow_send, flow_recv):
    rows, width = storage_ref.shape[1], storage_ref.shape[2]
    low = 1 << (width.bit_length() // 2)
    high = width // low
    here = lax.axis_index("basin")
    mine = lax.axis_index("tile")

    barrier = pltpu.get_barrier_semaphore()
    for step in range(1, nset):
        pl.semaphore_signal(barrier, inc=1, device_id={"tile": lax.rem(mine + step, nset)}, device_id_type=MESH)

    @pl.when(here > 0)
    def _():
        pl.semaphore_signal(barrier, inc=1, device_id={"basin": here - 1}, device_id_type=MESH)

    @pl.when(here < npos - 1)
    def _():
        pl.semaphore_signal(barrier, inc=1, device_id={"basin": here + 1}, device_id_type=MESH)

    steps = list(range(1, nset)) + [0]
    loads = []
    for order, step in enumerate(steps):
        owner = lax.rem(mine + step, nset)
        where = pl.ds(pl.multiple_of(owner * rows, rows), rows)
        group = []
        for at, (source, target) in enumerate(((cell_hbm, cell), (water_hbm, water), (frac_hbm, frac))):
            copy = pltpu.make_async_copy(source.at[0, where], target.at[order], tile_sem.at[order, at])
            copy.start()
            group.append(copy)
        loads.append(group)
    matrix_loads = []
    for chain in range(rows):
        copy = pltpu.make_async_copy(inverse_hbm.at[0, chain], inverse.at[chain], inverse_sem.at[chain])
        copy.start()
        matrix_loads.append(copy)

    same = lax.rem(iota((high * rows, low * rows), 0), rows) == lax.rem(iota((high * rows, low * rows), 1), rows)
    spread = (iota((low * rows, width), 0) // rows == lax.rem(iota((low * rows, width), 1), low)).astype(jnp.bfloat16)
    block = iota((rows, width), 1) // low

    def cell_sums(order):
        cells = cell[order]
        upper = (cells // low).astype(jnp.float32).astype(jnp.bfloat16)
        lower = lax.rem(cells, low).astype(jnp.float32).astype(jnp.bfloat16)
        head, tail = two_terms(frac[order] * water[order])
        zero = jnp.zeros_like(head)
        one = jnp.ones_like(head)
        picks = [upper == jnp.bfloat16(at) for at in range(high)]
        left = jnp.concatenate([jnp.where(pick, head, zero) for pick in picks] + [jnp.where(pick, tail, zero) for pick in picks], axis=0)
        right = jnp.concatenate([jnp.where(lower == jnp.bfloat16(at), one, zero) for at in range(low)], axis=0)
        both = lax.dot_general(left, right, NT, preferred_element_type=jnp.float32)
        crossed = jnp.where(same, both[: high * rows] + both[high * rows:], 0.0)
        head, tail = two_terms(crossed)
        packed = jnp.dot(jnp.concatenate([head, tail], axis=0), spread, preferred_element_type=jnp.float32)
        packed = packed[: high * rows] + packed[high * rows:]
        total = packed[:rows]
        for at in range(1, high):
            total = jnp.where(block == at, packed[at * rows:(at + 1) * rows], total)
        return total

    sends = []
    own = None
    for order, step in enumerate(steps):
        for copy in loads[order]:
            copy.wait()
        sums = cell_sums(order)
        if step == 0:
            own = sums
            continue
        part[step - 1] = sums
        if order == 0:
            pl.semaphore_wait(barrier, nset - 1 + jnp.minimum(here, 1) + jnp.minimum(npos - 1 - here, 1))
        copy = pltpu.make_async_remote_copy(
            src_ref=part.at[step - 1], dst_ref=arrived.at[step - 1],
            send_sem=part_send.at[step - 1], recv_sem=part_recv.at[step - 1],
            device_id={"tile": lax.rem(mine + step, nset)}, device_id_type=MESH)
        copy.start()
        sends.append(copy)

    for chain in range(rows):
        matrix_loads[chain].wait()
        head, tail = two_terms(inverse[chain])
        heads[chain] = head
        tails[chain] = tail

    row = iota((rows, width), 0)
    links = jnp.zeros((rows, width), jnp.int32)
    for chain in range(rows):
        links = jnp.where(row == chain, upstream_ref[0, chain], links)
    live = mask_ref[0].astype(jnp.float32)
    rates = kappa_ref[0]
    picked = [row == chain for chain in range(rows)]

    runoff = own
    for at, copy in enumerate(sends):
        copy.wait_recv()
        runoff = runoff + arrived[at]
    forcing = time_step * runoff

    def product(vector):
        head, tail = two_terms(vector)
        total = jnp.zeros((2 * rows, width), jnp.float32)
        zero = jnp.zeros_like(head)
        for chain in range(rows):
            upper = jnp.where(picked[chain], head, zero)
            left = jnp.concatenate([upper, jnp.where(picked[chain], tail, zero)], axis=0)
            total += lax.dot_general(left, heads[chain], NT, preferred_element_type=jnp.float32)
            total += lax.dot_general(left, tails[chain], NT, preferred_element_type=jnp.float32)
        return total[:rows] + total[rows:]

    @pl.when(here == 0)
    def _():
        inflow[...] = jnp.zeros_like(inflow)

    level = storage_ref[0]
    outflow = level
    for substep in range(SUBSTEPS):
        copy = pltpu.make_async_remote_copy(
            src_ref=flow.at[substep], dst_ref=inflow.at[substep],
            send_sem=flow_send.at[substep], recv_sem=flow_recv.at[substep],
            device_id={"basin": lax.rem(here + 1, npos)}, device_id_type=MESH)

        @pl.when(here > 0)
        def _():
            copy.wait_recv()

        came = inflow[substep]
        incoming = jnp.broadcast_to(came[:1], (rows, width))
        for chain in range(1, rows):
            incoming = jnp.where(links == chain, jnp.broadcast_to(came[chain:chain + 1], (rows, width)), incoming)
        wet = live * product(level + forcing + incoming)
        outflow = rates * wet
        level = wet - outflow

        @pl.when(here < npos - 1)
        def _():
            flow[substep] = outflow
            copy.start()

    level_ref[0] = level
    discharge_ref[0] = outflow

    for copy in sends:
        copy.wait_send()

    @pl.when(here < npos - 1)
    def _():
        for substep in range(SUBSTEPS):
            pltpu.make_async_remote_copy(
                src_ref=flow.at[substep], dst_ref=inflow.at[substep],
                send_sem=flow_send.at[substep], recv_sem=flow_recv.at[substep],
                device_id={"basin": lax.rem(here + 1, npos)}, device_id_type=MESH).wait_send()


def solution(mesh):
    npos, nset = mesh.shape["basin"], mesh.shape["tile"]

    def local(tile_water, tile_frac, tile_cell, storage, kappa, inverse, cell_mask, upstream):
        rows, width = storage.shape[1:]
        tiles = tile_water.shape[2]
        anywhere = pl.BlockSpec(memory_space=pl.ANY)
        vmem = pl.BlockSpec(memory_space=pltpu.VMEM)
        smem = pl.BlockSpec(memory_space=pltpu.SMEM)
        out = jax.ShapeDtypeStruct(storage.shape, jnp.float32)
        return pl.pallas_call(
            functools.partial(kernel, npos, nset),
            out_shape=(out, out),
            in_specs=[anywhere, anywhere, anywhere, vmem, vmem, anywhere, vmem, smem],
            out_specs=(vmem, vmem),
            scratch_shapes=[
                pltpu.VMEM((nset, rows, tiles), jnp.float32),
                pltpu.VMEM((nset, rows, tiles), jnp.float32),
                pltpu.VMEM((nset, rows, tiles), jnp.int32),
                pltpu.VMEM((rows, width, width), jnp.float32),
                pltpu.VMEM((rows, width, width), jnp.bfloat16),
                pltpu.VMEM((rows, width, width), jnp.bfloat16),
                pltpu.VMEM((nset - 1, rows, width), jnp.float32),
                pltpu.VMEM((nset - 1, rows, width), jnp.float32),
                pltpu.VMEM((SUBSTEPS, rows, width), jnp.float32),
                pltpu.VMEM((SUBSTEPS, rows, width), jnp.float32),
                pltpu.SemaphoreType.DMA((nset, 3)),
                pltpu.SemaphoreType.DMA((rows,)),
                pltpu.SemaphoreType.DMA((nset - 1,)),
                pltpu.SemaphoreType.DMA((nset - 1,)),
                pltpu.SemaphoreType.DMA((SUBSTEPS,)),
                pltpu.SemaphoreType.DMA((SUBSTEPS,)),
            ],
            compiler_params=pltpu.CompilerParams(collective_id=0, has_side_effects=True),
        )(tile_water, tile_frac, tile_cell, storage, kappa, inverse, cell_mask, upstream)

    tiled = P("basin", None, "tile")
    chain = P("basin", "tile", None)
    return jax.shard_map(
        local,
        mesh=mesh,
        in_specs=(tiled, tiled, tiled, chain, chain, P("basin", "tile", None, None), chain, P("basin", "tile")),
        out_specs=(chain, chain),
        check_vma=False,
    )
```

```python
import functools

import jax
import jax.numpy as jnp
from jax import lax
from jax.experimental import pallas as pl
from jax.experimental.pallas import tpu as pltpu
from jax.sharding import PartitionSpec as P

SUBSTEPS = 3
time_step = 0.5
MESH = pl.DeviceIdType.MESH
NT = (((1,), (1,)), ((), ()))


def two_terms(value):
    head = value.astype(jnp.bfloat16)
    return head, (value - head.astype(jnp.float32)).astype(jnp.bfloat16)


def iota(shape, axis):
    return lax.broadcasted_iota(jnp.int32, shape, axis)


def kernel(npos, nset, water_hbm, frac_hbm, cell_hbm, storage_ref, kappa_ref, inverse_hbm, mask_ref, upstream_ref,
           out_ref,
           water, frac, cell, inverse, heads, tails, part, arrived, flow, inflow,
           tile_sem, inverse_sem, part_send, part_recv, flow_send, flow_recv):
    rows, width = storage_ref.shape[1], storage_ref.shape[2]
    low = 1 << (width.bit_length() // 2)
    high = width // low
    here = lax.axis_index("basin")
    mine = lax.axis_index("tile")

    barrier = pltpu.get_barrier_semaphore()
    for step in range(1, nset):
        pl.semaphore_signal(barrier, inc=1, device_id={"tile": lax.rem(mine + step, nset)}, device_id_type=MESH)

    @pl.when(here > 0)
    def _():
        pl.semaphore_signal(barrier, inc=1, device_id={"basin": here - 1}, device_id_type=MESH)

    @pl.when(here < npos - 1)
    def _():
        pl.semaphore_signal(barrier, inc=1, device_id={"basin": here + 1}, device_id_type=MESH)

    steps = list(range(1, nset)) + [0]
    loads = []
    for order, step in enumerate(steps):
        owner = lax.rem(mine + step, nset)
        where = pl.ds(pl.multiple_of(owner * rows, rows), rows)
        group = []
        for at, (source, target) in enumerate(((cell_hbm, cell), (water_hbm, water), (frac_hbm, frac))):
            copy = pltpu.make_async_copy(source.at[0, where], target.at[order], tile_sem.at[order, at])
            copy.start()
            group.append(copy)
        loads.append(group)
    matrix_loads = []
    for chain in range(rows):
        copy = pltpu.make_async_copy(inverse_hbm.at[0, chain], inverse.at[chain], inverse_sem.at[chain])
        copy.start()
        matrix_loads.append(copy)

    same = lax.rem(iota((high * rows, low * rows), 0), rows) == lax.rem(iota((high * rows, low * rows), 1), rows)
    spread = (iota((low * rows, width), 0) // rows == lax.rem(iota((low * rows, width), 1), low)).astype(jnp.bfloat16)
    block = iota((rows, width), 1) // low

    def cell_sums(order):
        cells = cell[order]
        upper = (cells // low).astype(jnp.float32).astype(jnp.bfloat16)
        lower = lax.rem(cells, low).astype(jnp.float32).astype(jnp.bfloat16)
        head, tail = two_terms(frac[order] * water[order])
        zero = jnp.zeros_like(head)
        one = jnp.ones_like(head)
        picks = [upper == jnp.bfloat16(at) for at in range(high)]
        left = jnp.concatenate([jnp.where(pick, head, zero) for pick in picks] + [jnp.where(pick, tail, zero) for pick in picks], axis=0)
        right = jnp.concatenate([jnp.where(lower == jnp.bfloat16(at), one, zero) for at in range(low)], axis=0)
        both = lax.dot_general(left, right, NT, preferred_element_type=jnp.float32)
        crossed = jnp.where(same, both[: high * rows] + both[high * rows:], 0.0)
        head, tail = two_terms(crossed)
        packed = jnp.dot(jnp.concatenate([head, tail], axis=0), spread, preferred_element_type=jnp.float32)
        packed = packed[: high * rows] + packed[high * rows:]
        total = packed[:rows]
        for at in range(1, high):
            total = jnp.where(block == at, packed[at * rows:(at + 1) * rows], total)
        return total

    sends = []
    own = None
    for order, step in enumerate(steps):
        for copy in loads[order]:
            copy.wait()
        sums = cell_sums(order)
        if step == 0:
            own = sums
            continue
        part[step - 1] = sums
        if order == 0:
            pl.semaphore_wait(barrier, nset - 1 + jnp.minimum(here, 1) + jnp.minimum(npos - 1 - here, 1))
        copy = pltpu.make_async_remote_copy(
            src_ref=part.at[step - 1], dst_ref=arrived.at[step - 1],
            send_sem=part_send.at[step - 1], recv_sem=part_recv.at[step - 1],
            device_id={"tile": lax.rem(mine + step, nset)}, device_id_type=MESH)
        copy.start()
        sends.append(copy)

    for chain in range(rows):
        matrix_loads[chain].wait()
        head, tail = two_terms(inverse[chain].T)
        heads[chain] = head
        tails[chain] = tail

    row = iota((rows, width), 0)
    links = jnp.zeros((rows, width), jnp.int32)
    for chain in range(rows):
        links = jnp.where(row == chain, upstream_ref[0, chain], links)
    live = mask_ref[0].astype(jnp.float32)
    rates = kappa_ref[0]
    picked = [row == chain for chain in range(rows)]

    runoff = own
    for at, copy in enumerate(sends):
        copy.wait_recv()
        runoff = runoff + arrived[at]
    forcing = time_step * runoff

    def product(vector):
        head, tail = two_terms(vector)
        total = jnp.zeros((2 * rows, width), jnp.float32)
        zero = jnp.zeros_like(head)
        for chain in range(rows):
            upper = jnp.where(picked[chain], head, zero)
            left = jnp.concatenate([upper, jnp.where(picked[chain], tail, zero)], axis=0)
            total += jnp.dot(left, heads[chain], preferred_element_type=jnp.float32)
            total += jnp.dot(left, tails[chain], preferred_element_type=jnp.float32)
        return total[:rows] + total[rows:]

    @pl.when(here == 0)
    def _():
        inflow[...] = jnp.zeros_like(inflow)

    level = storage_ref[0]
    outflow = level
    for substep in range(SUBSTEPS):
        copy = pltpu.make_async_remote_copy(
            src_ref=flow.at[substep], dst_ref=inflow.at[substep],
            send_sem=flow_send.at[substep], recv_sem=flow_recv.at[substep],
            device_id={"basin": lax.rem(here + 1, npos)}, device_id_type=MESH)

        @pl.when(here > 0)
        def _():
            copy.wait_recv()

        came = inflow[substep]
        incoming = jnp.broadcast_to(came[:1], (rows, width))
        for chain in range(1, rows):
            incoming = jnp.where(links == chain, jnp.broadcast_to(came[chain:chain + 1], (rows, width)), incoming)
        wet = live * product(level + forcing + incoming)
        outflow = rates * wet
        level = wet - outflow

        @pl.when(here < npos - 1)
        def _():
            flow[substep] = outflow
            copy.start()

    out_ref[0] = level
    out_ref[1] = outflow

    for copy in sends:
        copy.wait_send()

    @pl.when(here < npos - 1)
    def _():
        for substep in range(SUBSTEPS):
            pltpu.make_async_remote_copy(
                src_ref=flow.at[substep], dst_ref=inflow.at[substep],
                send_sem=flow_send.at[substep], recv_sem=flow_recv.at[substep],
                device_id={"basin": lax.rem(here + 1, npos)}, device_id_type=MESH).wait_send()


def solution(mesh):
    npos, nset = mesh.shape["basin"], mesh.shape["tile"]

    def local(tile_water, tile_frac, tile_cell, storage, kappa, inverse, cell_mask, upstream):
        rows, width = storage.shape[1:]
        tiles = tile_water.shape[2]
        anywhere = pl.BlockSpec(memory_space=pl.ANY)
        vmem = pl.BlockSpec(memory_space=pltpu.VMEM)
        smem = pl.BlockSpec(memory_space=pltpu.SMEM)
        out = pl.pallas_call(
            functools.partial(kernel, npos, nset),
            out_shape=jax.ShapeDtypeStruct((2, rows, width), jnp.float32),
            in_specs=[anywhere, anywhere, anywhere, vmem, vmem, anywhere, vmem, smem],
            out_specs=vmem,
            scratch_shapes=[
                pltpu.VMEM((nset, rows, tiles), jnp.float32),
                pltpu.VMEM((nset, rows, tiles), jnp.float32),
                pltpu.VMEM((nset, rows, tiles), jnp.int32),
                pltpu.VMEM((rows, width, width), jnp.float32),
                pltpu.VMEM((rows, width, width), jnp.bfloat16),
                pltpu.VMEM((rows, width, width), jnp.bfloat16),
                pltpu.VMEM((nset - 1, rows, width), jnp.float32),
                pltpu.VMEM((nset - 1, rows, width), jnp.float32),
                pltpu.VMEM((SUBSTEPS, rows, width), jnp.float32),
                pltpu.VMEM((SUBSTEPS, rows, width), jnp.float32),
                pltpu.SemaphoreType.DMA((nset, 3)),
                pltpu.SemaphoreType.DMA((rows,)),
                pltpu.SemaphoreType.DMA((nset - 1,)),
                pltpu.SemaphoreType.DMA((nset - 1,)),
                pltpu.SemaphoreType.DMA((SUBSTEPS,)),
                pltpu.SemaphoreType.DMA((SUBSTEPS,)),
            ],
            compiler_params=pltpu.CompilerParams(collective_id=0, has_side_effects=True),
        )(tile_water, tile_frac, tile_cell, storage, kappa, inverse, cell_mask, upstream)
        return out[:1], out[1:]

    tiled = P("basin", None, "tile")
    chain = P("basin", "tile", None)
    return jax.shard_map(
        local,
        mesh=mesh,
        in_specs=(tiled, tiled, tiled, chain, chain, P("basin", "tile", None, None), chain, P("basin", "tile")),
        out_specs=(chain, chain),
        check_vma=False,
    )
```

```python
import functools

import jax
import jax.numpy as jnp
from jax import lax
from jax.experimental import pallas as pl
from jax.experimental.pallas import tpu as pltpu
from jax.sharding import PartitionSpec as P

SUBSTEPS = 3
time_step = 0.5
MESH = pl.DeviceIdType.MESH
NT = (((1,), (1,)), ((), ()))


def two_terms(value):
    head = value.astype(jnp.bfloat16)
    return head, (value - head.astype(jnp.float32)).astype(jnp.bfloat16)


def iota(shape, axis):
    return lax.broadcasted_iota(jnp.int32, shape, axis)


def kernel(npos, nset, water_hbm, frac_hbm, cell_hbm, storage_ref, kappa_ref, inverse_hbm, mask_ref, upstream_ref,
           out_ref,
           water, frac, cell, inverse, heads, tails, part, arrived, flow, inflow,
           tile_sem, inverse_sem, part_send, part_recv, flow_send, flow_recv):
    rows, width = storage_ref.shape[1], storage_ref.shape[2]
    low = 1 << (width.bit_length() // 2)
    high = width // low
    here = lax.axis_index("basin")
    mine = lax.axis_index("tile")

    barrier = pltpu.get_barrier_semaphore()
    for step in range(1, nset):
        pl.semaphore_signal(barrier, inc=1, device_id={"tile": lax.rem(mine + step, nset)}, device_id_type=MESH)

    @pl.when(here > 0)
    def _():
        pl.semaphore_signal(barrier, inc=1, device_id={"basin": here - 1}, device_id_type=MESH)

    @pl.when(here < npos - 1)
    def _():
        pl.semaphore_signal(barrier, inc=1, device_id={"basin": here + 1}, device_id_type=MESH)

    steps = list(range(1, nset)) + [0]
    loads = []
    for order, step in enumerate(steps):
        owner = lax.rem(mine + step, nset)
        where = pl.ds(pl.multiple_of(owner * rows, rows), rows)
        group = []
        for at, (source, target) in enumerate(((cell_hbm, cell), (water_hbm, water), (frac_hbm, frac))):
            copy = pltpu.make_async_copy(source.at[0, where], target.at[order], tile_sem.at[order, at])
            copy.start()
            group.append(copy)
        loads.append(group)
    matrix_loads = []
    for chain in range(rows):
        copy = pltpu.make_async_copy(inverse_hbm.at[0, chain], inverse.at[chain], inverse_sem.at[chain])
        copy.start()
        matrix_loads.append(copy)

    same = lax.rem(iota((high * rows, low * rows), 0), rows) == lax.rem(iota((high * rows, low * rows), 1), rows)
    spread = (iota((low * rows, width), 0) // rows == lax.rem(iota((low * rows, width), 1), low)).astype(jnp.bfloat16)
    block = iota((rows, width), 1) // low

    def cell_sums(order):
        cells = cell[order]
        upper = (cells // low).astype(jnp.float32).astype(jnp.bfloat16)
        lower = lax.rem(cells, low).astype(jnp.float32).astype(jnp.bfloat16)
        head, tail = two_terms(frac[order] * water[order])
        zero = jnp.zeros_like(head)
        one = jnp.ones_like(head)
        picks = [upper == jnp.bfloat16(at) for at in range(high)]
        left = jnp.concatenate([jnp.where(pick, head, zero) for pick in picks] + [jnp.where(pick, tail, zero) for pick in picks], axis=0)
        right = jnp.concatenate([jnp.where(lower == jnp.bfloat16(at), one, zero) for at in range(low)], axis=0)
        both = lax.dot_general(left, right, NT, preferred_element_type=jnp.float32)
        crossed = jnp.where(same, both[: high * rows] + both[high * rows:], 0.0)
        head, tail = two_terms(crossed)
        packed = jnp.dot(jnp.concatenate([head, tail], axis=0), spread, preferred_element_type=jnp.float32)
        packed = packed[: high * rows] + packed[high * rows:]
        total = packed[:rows]
        for at in range(1, high):
            total = jnp.where(block == at, packed[at * rows:(at + 1) * rows], total)
        return total

    sends = []
    own = None
    for order, step in enumerate(steps):
        for copy in loads[order]:
            copy.wait()
        sums = cell_sums(order)
        if step == 0:
            own = sums
            continue
        part[step - 1] = sums
        if order == 0:
            pl.semaphore_wait(barrier, nset - 1 + jnp.minimum(here, 1) + jnp.minimum(npos - 1 - here, 1))
        copy = pltpu.make_async_remote_copy(
            src_ref=part.at[step - 1], dst_ref=arrived.at[step - 1],
            send_sem=part_send.at[step - 1], recv_sem=part_recv.at[step - 1],
            device_id={"tile": lax.rem(mine + step, nset)}, device_id_type=MESH)
        copy.start()
        sends.append(copy)

    for chain in range(rows):
        matrix_loads[chain].wait()
        head, tail = two_terms(inverse[chain].T)
        heads[chain] = head
        tails[chain] = tail

    row = iota((rows, width), 0)
    links = jnp.zeros((rows, width), jnp.int32)
    for chain in range(rows):
        links = jnp.where(row == chain, upstream_ref[0, chain], links)
    live = mask_ref[0].astype(jnp.float32)
    rates = kappa_ref[0]
    half = rows // 2
    picked = [lax.rem(iota((2 * half, width), 0), half) == chain for chain in range(half)]

    runoff = own
    for at, copy in enumerate(sends):
        copy.wait_recv()
        runoff = runoff + arrived[at]
    forcing = time_step * runoff

    def product(vector):
        head = vector.astype(jnp.bfloat16).astype(jnp.float32)
        tail = vector - head
        starts = range(0, rows, half)
        lefts = [jnp.concatenate([head[start:start + half], tail[start:start + half]], axis=0).astype(jnp.bfloat16) for start in starts]
        totals = [jnp.zeros((2 * half, width), jnp.float32) for _ in starts]
        for chain in range(half):
            for at, start in enumerate(starts):
                single = jnp.where(picked[chain], lefts[at], jnp.zeros_like(lefts[at]))
                totals[at] += jnp.dot(single, heads[start + chain], preferred_element_type=jnp.float32)
            for at, start in enumerate(starts):
                single = jnp.where(picked[chain], lefts[at], jnp.zeros_like(lefts[at]))
                totals[at] += jnp.dot(single, tails[start + chain], preferred_element_type=jnp.float32)
        return jnp.concatenate([total[:half] + total[half:] for total in totals], axis=0)

    @pl.when(here == 0)
    def _():
        inflow[...] = jnp.zeros_like(inflow)

    level = storage_ref[0]
    outflow = level
    for substep in range(SUBSTEPS):
        copy = pltpu.make_async_remote_copy(
            src_ref=flow.at[substep], dst_ref=inflow.at[substep],
            send_sem=flow_send.at[substep], recv_sem=flow_recv.at[substep],
            device_id={"basin": lax.rem(here + 1, npos)}, device_id_type=MESH)

        @pl.when(here > 0)
        def _():
            copy.wait_recv()

        came = inflow[substep]
        incoming = jnp.broadcast_to(came[:1], (rows, width))
        for chain in range(1, rows):
            incoming = jnp.where(links == chain, jnp.broadcast_to(came[chain:chain + 1], (rows, width)), incoming)
        wet = live * product(level + forcing + incoming)
        outflow = rates * wet
        level = wet - outflow

        @pl.when(here < npos - 1)
        def _():
            flow[substep] = outflow
            copy.start()

    out_ref[0] = level
    out_ref[1] = outflow

    for copy in sends:
        copy.wait_send()

    @pl.when(here < npos - 1)
    def _():
        for substep in range(SUBSTEPS):
            pltpu.make_async_remote_copy(
                src_ref=flow.at[substep], dst_ref=inflow.at[substep],
                send_sem=flow_send.at[substep], recv_sem=flow_recv.at[substep],
                device_id={"basin": lax.rem(here + 1, npos)}, device_id_type=MESH).wait_send()


def solution(mesh):
    npos, nset = mesh.shape["basin"], mesh.shape["tile"]

    def local(tile_water, tile_frac, tile_cell, storage, kappa, inverse, cell_mask, upstream):
        rows, width = storage.shape[1:]
        tiles = tile_water.shape[2]
        anywhere = pl.BlockSpec(memory_space=pl.ANY)
        vmem = pl.BlockSpec(memory_space=pltpu.VMEM)
        smem = pl.BlockSpec(memory_space=pltpu.SMEM)
        out = pl.pallas_call(
            functools.partial(kernel, npos, nset),
            out_shape=jax.ShapeDtypeStruct((2, rows, width), jnp.float32),
            in_specs=[anywhere, anywhere, anywhere, vmem, vmem, anywhere, vmem, smem],
            out_specs=vmem,
            scratch_shapes=[
                pltpu.VMEM((nset, rows, tiles), jnp.float32),
                pltpu.VMEM((nset, rows, tiles), jnp.float32),
                pltpu.VMEM((nset, rows, tiles), jnp.int32),
                pltpu.VMEM((rows, width, width), jnp.float32),
                pltpu.VMEM((rows, width, width), jnp.bfloat16),
                pltpu.VMEM((rows, width, width), jnp.bfloat16),
                pltpu.VMEM((nset - 1, rows, width), jnp.float32),
                pltpu.VMEM((nset - 1, rows, width), jnp.float32),
                pltpu.VMEM((SUBSTEPS, rows, width), jnp.float32),
                pltpu.VMEM((SUBSTEPS, rows, width), jnp.float32),
                pltpu.SemaphoreType.DMA((nset, 3)),
                pltpu.SemaphoreType.DMA((rows,)),
                pltpu.SemaphoreType.DMA((nset - 1,)),
                pltpu.SemaphoreType.DMA((nset - 1,)),
                pltpu.SemaphoreType.DMA((SUBSTEPS,)),
                pltpu.SemaphoreType.DMA((SUBSTEPS,)),
            ],
            compiler_params=pltpu.CompilerParams(collective_id=0, has_side_effects=True),
        )(tile_water, tile_frac, tile_cell, storage, kappa, inverse, cell_mask, upstream)
        return out[:1], out[1:]

    tiled = P("basin", None, "tile")
    chain = P("basin", "tile", None)
    return jax.shard_map(
        local,
        mesh=mesh,
        in_specs=(tiled, tiled, tiled, chain, chain, P("basin", "tile", None, None), chain, P("basin", "tile")),
        out_specs=(chain, chain),
        check_vma=False,
    )
```

```python
import functools

import jax
import jax.numpy as jnp
from jax import lax
from jax.experimental import pallas as pl
from jax.experimental.pallas import tpu as pltpu
from jax.sharding import PartitionSpec as P

SUBSTEPS = 3
time_step = 0.5
MESH = pl.DeviceIdType.MESH
NT = (((1,), (1,)), ((), ()))


def two_terms(value):
    head = value.astype(jnp.bfloat16)
    return head, (value - head.astype(jnp.float32)).astype(jnp.bfloat16)


def iota(shape, axis):
    return lax.broadcasted_iota(jnp.int32, shape, axis)


def kernel(npos, nset, water_hbm, frac_hbm, cell_hbm, storage_hbm, kappa_hbm, inverse_hbm, mask_hbm, upstream_hbm,
           out_ref,
           storage_ref, kappa_ref, mask_ref, upstream_ref, water, frac, cell, inverse, heads, tails, part, arrived, flow, inflow,
           small_sem, tile_sem, inverse_sem, part_send, part_recv, flow_send, flow_recv):
    rows, width = storage_ref.shape[1], storage_ref.shape[2]
    low = 1 << (width.bit_length() // 2)
    high = width // low
    here = lax.axis_index("basin")
    mine = lax.axis_index("tile")

    barrier = pltpu.get_barrier_semaphore()
    for step in range(1, nset):
        pl.semaphore_signal(barrier, inc=1, device_id={"tile": lax.rem(mine + step, nset)}, device_id_type=MESH)

    @pl.when(here > 0)
    def _():
        pl.semaphore_signal(barrier, inc=1, device_id={"basin": here - 1}, device_id_type=MESH)

    @pl.when(here < npos - 1)
    def _():
        pl.semaphore_signal(barrier, inc=1, device_id={"basin": here + 1}, device_id_type=MESH)

    steps = list(range(1, nset)) + [0]
    loads = []
    for order, step in enumerate(steps):
        owner = lax.rem(mine + step, nset)
        where = pl.ds(pl.multiple_of(owner * rows, rows), rows)
        group = []
        for at, (source, target) in enumerate(((cell_hbm, cell), (water_hbm, water), (frac_hbm, frac))):
            copy = pltpu.make_async_copy(source.at[0, where], target.at[order], tile_sem.at[order, at])
            copy.start()
            group.append(copy)
        loads.append(group)
    small_loads = []
    for at, (source, target) in enumerate(((storage_hbm, storage_ref), (kappa_hbm, kappa_ref), (mask_hbm, mask_ref), (upstream_hbm, upstream_ref))):
        copy = pltpu.make_async_copy(source, target, small_sem.at[at])
        copy.start()
        small_loads.append(copy)
    matrix_loads = []
    for chain in range(rows):
        copy = pltpu.make_async_copy(inverse_hbm.at[0, chain], inverse.at[chain], inverse_sem.at[chain])
        copy.start()
        matrix_loads.append(copy)

    same = lax.rem(iota((high * rows, low * rows), 0), rows) == lax.rem(iota((high * rows, low * rows), 1), rows)
    spread = (iota((low * rows, width), 0) // rows == lax.rem(iota((low * rows, width), 1), low)).astype(jnp.bfloat16)
    block = iota((rows, width), 1) // low

    def cell_sums(order):
        cells = cell[order]
        upper = (cells // low).astype(jnp.float32).astype(jnp.bfloat16)
        lower = lax.rem(cells, low).astype(jnp.float32).astype(jnp.bfloat16)
        head, tail = two_terms(frac[order] * water[order])
        zero = jnp.zeros_like(head)
        one = jnp.ones_like(head)
        picks = [upper == jnp.bfloat16(at) for at in range(high)]
        left = jnp.concatenate([jnp.where(pick, head, zero) for pick in picks] + [jnp.where(pick, tail, zero) for pick in picks], axis=0)
        right = jnp.concatenate([jnp.where(lower == jnp.bfloat16(at), one, zero) for at in range(low)], axis=0)
        both = lax.dot_general(left, right, NT, preferred_element_type=jnp.float32)
        crossed = jnp.where(same, both[: high * rows] + both[high * rows:], 0.0)
        head, tail = two_terms(crossed)
        packed = jnp.dot(jnp.concatenate([head, tail], axis=0), spread, preferred_element_type=jnp.float32)
        packed = packed[: high * rows] + packed[high * rows:]
        total = packed[:rows]
        for at in range(1, high):
            total = jnp.where(block == at, packed[at * rows:(at + 1) * rows], total)
        return total

    sends = []
    own = None
    for order, step in enumerate(steps):
        for copy in loads[order]:
            copy.wait()
        sums = cell_sums(order)
        if step == 0:
            own = sums
            continue
        part[step - 1] = sums
        if order == 0:
            pl.semaphore_wait(barrier, nset - 1 + jnp.minimum(here, 1) + jnp.minimum(npos - 1 - here, 1))
        copy = pltpu.make_async_remote_copy(
            src_ref=part.at[step - 1], dst_ref=arrived.at[step - 1],
            send_sem=part_send.at[step - 1], recv_sem=part_recv.at[step - 1],
            device_id={"tile": lax.rem(mine + step, nset)}, device_id_type=MESH)
        copy.start()
        sends.append(copy)

    for chain in range(rows):
        matrix_loads[chain].wait()
        head, tail = two_terms(inverse[chain].T)
        heads[chain] = head
        tails[chain] = tail

    for copy in small_loads:
        copy.wait()
    row = iota((rows, width), 0)
    links = jnp.zeros((rows, width), jnp.int32)
    for chain in range(rows):
        links = jnp.where(row == chain, upstream_ref[0, chain], links)
    live = mask_ref[0].astype(jnp.float32)
    rates = kappa_ref[0]
    half = rows // 2
    picked = [lax.rem(iota((2 * half, width), 0), half) == chain for chain in range(half)]

    runoff = own
    for at, copy in enumerate(sends):
        copy.wait_recv()
        runoff = runoff + arrived[at]
    forcing = time_step * runoff

    def product(vector):
        head = vector.astype(jnp.bfloat16).astype(jnp.float32)
        tail = vector - head
        starts = range(0, rows, half)
        lefts = [jnp.concatenate([head[start:start + half], tail[start:start + half]], axis=0).astype(jnp.bfloat16) for start in starts]
        totals = [jnp.zeros((2 * half, width), jnp.float32) for _ in starts]
        for chain in range(half):
            for at, start in enumerate(starts):
                single = jnp.where(picked[chain], lefts[at], jnp.zeros_like(lefts[at]))
                totals[at] += jnp.dot(single, heads[start + chain], preferred_element_type=jnp.float32)
            for at, start in enumerate(starts):
                single = jnp.where(picked[chain], lefts[at], jnp.zeros_like(lefts[at]))
                totals[at] += jnp.dot(single, tails[start + chain], preferred_element_type=jnp.float32)
        return jnp.concatenate([total[:half] + total[half:] for total in totals], axis=0)

    @pl.when(here == 0)
    def _():
        inflow[...] = jnp.zeros_like(inflow)

    level = storage_ref[0]
    outflow = level
    for substep in range(SUBSTEPS):
        copy = pltpu.make_async_remote_copy(
            src_ref=flow.at[substep], dst_ref=inflow.at[substep],
            send_sem=flow_send.at[substep], recv_sem=flow_recv.at[substep],
            device_id={"basin": lax.rem(here + 1, npos)}, device_id_type=MESH)

        @pl.when(here > 0)
        def _():
            copy.wait_recv()

        came = inflow[substep]
        incoming = jnp.broadcast_to(came[:1], (rows, width))
        for chain in range(1, rows):
            incoming = jnp.where(links == chain, jnp.broadcast_to(came[chain:chain + 1], (rows, width)), incoming)
        wet = live * product(level + forcing + incoming)
        outflow = rates * wet
        level = wet - outflow

        @pl.when(here < npos - 1)
        def _():
            flow[substep] = outflow
            copy.start()

    out_ref[0] = level
    out_ref[1] = outflow

    for copy in sends:
        copy.wait_send()

    @pl.when(here < npos - 1)
    def _():
        for substep in range(SUBSTEPS):
            pltpu.make_async_remote_copy(
                src_ref=flow.at[substep], dst_ref=inflow.at[substep],
                send_sem=flow_send.at[substep], recv_sem=flow_recv.at[substep],
                device_id={"basin": lax.rem(here + 1, npos)}, device_id_type=MESH).wait_send()


def solution(mesh):
    npos, nset = mesh.shape["basin"], mesh.shape["tile"]

    def local(tile_water, tile_frac, tile_cell, storage, kappa, inverse, cell_mask, upstream):
        rows, width = storage.shape[1:]
        tiles = tile_water.shape[2]
        anywhere = pl.BlockSpec(memory_space=pl.ANY)
        vmem = pl.BlockSpec(memory_space=pltpu.VMEM)
        out = pl.pallas_call(
            functools.partial(kernel, npos, nset),
            out_shape=jax.ShapeDtypeStruct((2, rows, width), jnp.float32),
            in_specs=[anywhere] * 8,
            out_specs=vmem,
            scratch_shapes=[
                pltpu.VMEM(storage.shape, jnp.float32),
                pltpu.VMEM(kappa.shape, jnp.float32),
                pltpu.VMEM(cell_mask.shape, jnp.int32),
                pltpu.SMEM(upstream.shape, jnp.int32),
                pltpu.VMEM((nset, rows, tiles), jnp.float32),
                pltpu.VMEM((nset, rows, tiles), jnp.float32),
                pltpu.VMEM((nset, rows, tiles), jnp.int32),
                pltpu.VMEM((rows, width, width), jnp.float32),
                pltpu.VMEM((rows, width, width), jnp.bfloat16),
                pltpu.VMEM((rows, width, width), jnp.bfloat16),
                pltpu.VMEM((nset - 1, rows, width), jnp.float32),
                pltpu.VMEM((nset - 1, rows, width), jnp.float32),
                pltpu.VMEM((SUBSTEPS, rows, width), jnp.float32),
                pltpu.VMEM((SUBSTEPS, rows, width), jnp.float32),
                pltpu.SemaphoreType.DMA((4,)),
                pltpu.SemaphoreType.DMA((nset, 3)),
                pltpu.SemaphoreType.DMA((rows,)),
                pltpu.SemaphoreType.DMA((nset - 1,)),
                pltpu.SemaphoreType.DMA((nset - 1,)),
                pltpu.SemaphoreType.DMA((SUBSTEPS,)),
                pltpu.SemaphoreType.DMA((SUBSTEPS,)),
            ],
            compiler_params=pltpu.CompilerParams(collective_id=0, has_side_effects=True),
        )(tile_water, tile_frac, tile_cell, storage, kappa, inverse, cell_mask, upstream)
        return out[:1], out[1:]

    tiled = P("basin", None, "tile")
    chain = P("basin", "tile", None)
    return jax.shard_map(
        local,
        mesh=mesh,
        in_specs=(tiled, tiled, tiled, chain, chain, P("basin", "tile", None, None), chain, P("basin", "tile")),
        out_specs=(chain, chain),
        check_vma=False,
    )
```

```python
import functools

import jax
import jax.numpy as jnp
from jax import lax
from jax.experimental import pallas as pl
from jax.experimental.pallas import tpu as pltpu
from jax.sharding import PartitionSpec as P

SUBSTEPS = 3
time_step = 0.5
MESH = pl.DeviceIdType.MESH
NT = (((1,), (1,)), ((), ()))


def two_terms(value):
    head = value.astype(jnp.bfloat16)
    return head, (value - head.astype(jnp.float32)).astype(jnp.bfloat16)


def iota(shape, axis):
    return lax.broadcasted_iota(jnp.int32, shape, axis)


def kernel(npos, nset, water_hbm, frac_hbm, cell_hbm, storage_hbm, kappa_hbm, inverse_hbm, mask_hbm, upstream_hbm,
           out_ref,
           storage_ref, kappa_ref, mask_ref, upstream_ref, water, frac, cell, inverse, heads, tails, part, arrived, flow, inflow,
           small_sem, tile_sem, inverse_sem, part_send, part_recv, flow_send, flow_recv):
    rows, width = storage_ref.shape[1], storage_ref.shape[2]
    low = 1 << (width.bit_length() // 2)
    high = width // low
    here = lax.axis_index("basin")
    mine = lax.axis_index("tile")

    barrier = pltpu.get_barrier_semaphore()
    for step in range(1, nset):
        pl.semaphore_signal(barrier, inc=1, device_id={"tile": lax.rem(mine + step, nset)}, device_id_type=MESH)

    @pl.when(here > 0)
    def _():
        pl.semaphore_signal(barrier, inc=1, device_id={"basin": here - 1}, device_id_type=MESH)

    @pl.when(here < npos - 1)
    def _():
        pl.semaphore_signal(barrier, inc=1, device_id={"basin": here + 1}, device_id_type=MESH)

    steps = list(range(1, nset)) + [0]
    loads = []
    for order, step in enumerate(steps):
        owner = lax.rem(mine + step, nset)
        where = pl.ds(pl.multiple_of(owner * rows, rows), rows)
        group = []
        for at, (source, target) in enumerate(((cell_hbm, cell), (water_hbm, water), (frac_hbm, frac))):
            copy = pltpu.make_async_copy(source.at[0, where], target.at[order], tile_sem.at[order, at])
            copy.start()
            group.append(copy)
        loads.append(group)
    small_loads = []
    for at, (source, target) in enumerate(((storage_hbm, storage_ref), (kappa_hbm, kappa_ref), (mask_hbm, mask_ref), (upstream_hbm, upstream_ref))):
        copy = pltpu.make_async_copy(source, target, small_sem.at[at])
        copy.start()
        small_loads.append(copy)
    matrix_loads = []
    for chain in range(rows):
        copy = pltpu.make_async_copy(inverse_hbm.at[0, chain], inverse.at[chain], inverse_sem.at[chain])
        copy.start()
        matrix_loads.append(copy)

    same = lax.rem(iota((high * rows, low * rows), 0), rows) == lax.rem(iota((high * rows, low * rows), 1), rows)
    spread = (iota((low * rows, width), 0) // rows == lax.rem(iota((low * rows, width), 1), low)).astype(jnp.bfloat16)
    block = iota((rows, width), 1) // low

    def cell_sums(order):
        cells = cell[order]
        upper = (cells // low).astype(jnp.float32).astype(jnp.bfloat16)
        lower = lax.rem(cells, low).astype(jnp.float32).astype(jnp.bfloat16)
        head, tail = two_terms(frac[order] * water[order])
        zero = jnp.zeros_like(head)
        one = jnp.ones_like(head)
        picks = [upper == jnp.bfloat16(at) for at in range(high)]
        left = jnp.concatenate([jnp.where(pick, head, zero) for pick in picks] + [jnp.where(pick, tail, zero) for pick in picks], axis=0)
        right = jnp.concatenate([jnp.where(lower == jnp.bfloat16(at), one, zero) for at in range(low)], axis=0)
        both = lax.dot_general(left, right, NT, preferred_element_type=jnp.float32)
        crossed = jnp.where(same, both[: high * rows] + both[high * rows:], 0.0)
        head, tail = two_terms(crossed)
        packed = jnp.dot(jnp.concatenate([head, tail], axis=0), spread, preferred_element_type=jnp.float32)
        packed = packed[: high * rows] + packed[high * rows:]
        total = packed[:rows]
        for at in range(1, high):
            total = jnp.where(block == at, packed[at * rows:(at + 1) * rows], total)
        return total

    sends = []
    own = None
    for order, step in enumerate(steps):
        for copy in loads[order]:
            copy.wait()
        if step == 0:
            for copy in matrix_loads + small_loads:
                copy.wait()
            own = cell_sums(order)
            for chain in range(rows):
                head, tail = two_terms(inverse[chain].T)
                heads[chain] = head
                tails[chain] = tail
            continue
        sums = cell_sums(order)
        part[step - 1] = sums
        if order == 0:
            pl.semaphore_wait(barrier, nset - 1 + jnp.minimum(here, 1) + jnp.minimum(npos - 1 - here, 1))
        copy = pltpu.make_async_remote_copy(
            src_ref=part.at[step - 1], dst_ref=arrived.at[step - 1],
            send_sem=part_send.at[step - 1], recv_sem=part_recv.at[step - 1],
            device_id={"tile": lax.rem(mine + step, nset)}, device_id_type=MESH)
        copy.start()
        sends.append(copy)

    row = iota((rows, width), 0)
    links = jnp.zeros((rows, width), jnp.int32)
    for chain in range(rows):
        links = jnp.where(row == chain, upstream_ref[0, chain], links)
    live = mask_ref[0].astype(jnp.float32)
    rates = kappa_ref[0]
    half = rows // 2
    picked = [lax.rem(iota((2 * half, width), 0), half) == chain for chain in range(half)]

    runoff = own
    for at, copy in enumerate(sends):
        copy.wait_recv()
        runoff = runoff + arrived[at]
    forcing = time_step * runoff

    def product(vector):
        head = vector.astype(jnp.bfloat16).astype(jnp.float32)
        tail = vector - head
        starts = range(0, rows, half)
        lefts = [jnp.concatenate([head[start:start + half], tail[start:start + half]], axis=0).astype(jnp.bfloat16) for start in starts]
        totals = [jnp.zeros((2 * half, width), jnp.float32) for _ in starts]
        for chain in range(half):
            for at, start in enumerate(starts):
                single = jnp.where(picked[chain], lefts[at], jnp.zeros_like(lefts[at]))
                totals[at] += jnp.dot(single, heads[start + chain], preferred_element_type=jnp.float32)
            for at, start in enumerate(starts):
                single = jnp.where(picked[chain], lefts[at], jnp.zeros_like(lefts[at]))
                totals[at] += jnp.dot(single, tails[start + chain], preferred_element_type=jnp.float32)
        return jnp.concatenate([total[:half] + total[half:] for total in totals], axis=0)

    @pl.when(here == 0)
    def _():
        inflow[...] = jnp.zeros_like(inflow)

    level = storage_ref[0]
    outflow = level
    for substep in range(SUBSTEPS):
        copy = pltpu.make_async_remote_copy(
            src_ref=flow.at[substep], dst_ref=inflow.at[substep],
            send_sem=flow_send.at[substep], recv_sem=flow_recv.at[substep],
            device_id={"basin": lax.rem(here + 1, npos)}, device_id_type=MESH)

        @pl.when(here > 0)
        def _():
            copy.wait_recv()

        came = inflow[substep]
        incoming = jnp.broadcast_to(came[:1], (rows, width))
        for chain in range(1, rows):
            incoming = jnp.where(links == chain, jnp.broadcast_to(came[chain:chain + 1], (rows, width)), incoming)
        wet = live * product(level + forcing + incoming)
        outflow = rates * wet
        level = wet - outflow

        @pl.when(here < npos - 1)
        def _():
            flow[substep] = outflow
            copy.start()

    out_ref[0] = level
    out_ref[1] = outflow

    for copy in sends:
        copy.wait_send()

    @pl.when(here < npos - 1)
    def _():
        for substep in range(SUBSTEPS):
            pltpu.make_async_remote_copy(
                src_ref=flow.at[substep], dst_ref=inflow.at[substep],
                send_sem=flow_send.at[substep], recv_sem=flow_recv.at[substep],
                device_id={"basin": lax.rem(here + 1, npos)}, device_id_type=MESH).wait_send()


def solution(mesh):
    npos, nset = mesh.shape["basin"], mesh.shape["tile"]

    def local(tile_water, tile_frac, tile_cell, storage, kappa, inverse, cell_mask, upstream):
        rows, width = storage.shape[1:]
        tiles = tile_water.shape[2]
        anywhere = pl.BlockSpec(memory_space=pl.ANY)
        vmem = pl.BlockSpec(memory_space=pltpu.VMEM)
        out = pl.pallas_call(
            functools.partial(kernel, npos, nset),
            out_shape=jax.ShapeDtypeStruct((2, rows, width), jnp.float32),
            in_specs=[anywhere] * 8,
            out_specs=vmem,
            scratch_shapes=[
                pltpu.VMEM(storage.shape, jnp.float32),
                pltpu.VMEM(kappa.shape, jnp.float32),
                pltpu.VMEM(cell_mask.shape, jnp.int32),
                pltpu.SMEM(upstream.shape, jnp.int32),
                pltpu.VMEM((nset, rows, tiles), jnp.float32),
                pltpu.VMEM((nset, rows, tiles), jnp.float32),
                pltpu.VMEM((nset, rows, tiles), jnp.int32),
                pltpu.VMEM((rows, width, width), jnp.float32),
                pltpu.VMEM((rows, width, width), jnp.bfloat16),
                pltpu.VMEM((rows, width, width), jnp.bfloat16),
                pltpu.VMEM((nset - 1, rows, width), jnp.float32),
                pltpu.VMEM((nset - 1, rows, width), jnp.float32),
                pltpu.VMEM((SUBSTEPS, rows, width), jnp.float32),
                pltpu.VMEM((SUBSTEPS, rows, width), jnp.float32),
                pltpu.SemaphoreType.DMA((4,)),
                pltpu.SemaphoreType.DMA((nset, 3)),
                pltpu.SemaphoreType.DMA((rows,)),
                pltpu.SemaphoreType.DMA((nset - 1,)),
                pltpu.SemaphoreType.DMA((nset - 1,)),
                pltpu.SemaphoreType.DMA((SUBSTEPS,)),
                pltpu.SemaphoreType.DMA((SUBSTEPS,)),
            ],
            compiler_params=pltpu.CompilerParams(collective_id=0, has_side_effects=True),
        )(tile_water, tile_frac, tile_cell, storage, kappa, inverse, cell_mask, upstream)
        return out[:1], out[1:]

    tiled = P("basin", None, "tile")
    chain = P("basin", "tile", None)
    return jax.shard_map(
        local,
        mesh=mesh,
        in_specs=(tiled, tiled, tiled, chain, chain, P("basin", "tile", None, None), chain, P("basin", "tile")),
        out_specs=(chain, chain),
        check_vma=False,
    )
```

```python
import functools

import jax
import jax.numpy as jnp
from jax import lax
from jax.experimental import pallas as pl
from jax.experimental.pallas import tpu as pltpu
from jax.sharding import PartitionSpec as P

SUBSTEPS = 3
time_step = 0.5
MESH = pl.DeviceIdType.MESH
NT = (((1,), (1,)), ((), ()))


def two_terms(value):
    head = value.astype(jnp.bfloat16)
    return head, (value - head.astype(jnp.float32)).astype(jnp.bfloat16)


def iota(shape, axis):
    return lax.broadcasted_iota(jnp.int32, shape, axis)


def kernel(npos, nset, water_hbm, frac_hbm, cell_hbm, storage_hbm, kappa_hbm, inverse_hbm, mask_hbm, upstream_hbm,
           out_ref,
           storage_ref, kappa_ref, mask_ref, upstream_ref, water, frac, cell, inverse, heads, tails, part, arrived, flow, inflow,
           small_sem, tile_sem, inverse_sem, part_send, part_recv, flow_send, flow_recv):
    rows, width = storage_ref.shape[1], storage_ref.shape[2]
    low = 1 << (width.bit_length() // 2)
    high = width // low
    here = lax.axis_index("basin")
    mine = lax.axis_index("tile")

    barrier = pltpu.get_barrier_semaphore()
    for step in range(1, nset):
        pl.semaphore_signal(barrier, inc=1, device_id={"tile": lax.rem(mine + step, nset)}, device_id_type=MESH)

    @pl.when(here > 0)
    def _():
        pl.semaphore_signal(barrier, inc=1, device_id={"basin": here - 1}, device_id_type=MESH)

    @pl.when(here < npos - 1)
    def _():
        pl.semaphore_signal(barrier, inc=1, device_id={"basin": here + 1}, device_id_type=MESH)

    steps = list(range(1, nset)) + [0]
    loads = []
    for order, step in enumerate(steps):
        owner = lax.rem(mine + step, nset)
        where = pl.ds(pl.multiple_of(owner * rows, rows), rows)
        group = []
        for at, (source, target) in enumerate(((cell_hbm, cell), (water_hbm, water), (frac_hbm, frac))):
            copy = pltpu.make_async_copy(source.at[0, where], target.at[order], tile_sem.at[order, at])
            copy.start()
            group.append(copy)
        loads.append(group)
    small_loads = []
    for at, (source, target) in enumerate(((storage_hbm, storage_ref), (kappa_hbm, kappa_ref), (mask_hbm, mask_ref), (upstream_hbm, upstream_ref))):
        copy = pltpu.make_async_copy(source, target, small_sem.at[at])
        copy.start()
        small_loads.append(copy)
    matrix_loads = []
    for chain in range(rows):
        copy = pltpu.make_async_copy(inverse_hbm.at[0, chain], inverse.at[chain], inverse_sem.at[chain])
        copy.start()
        matrix_loads.append(copy)

    same = lax.rem(iota((high * rows, low * rows), 0), rows) == lax.rem(iota((high * rows, low * rows), 1), rows)
    spread = (iota((low * rows, width), 0) // rows == lax.rem(iota((low * rows, width), 1), low)).astype(jnp.bfloat16)
    block = iota((rows, width), 1) // low

    def cell_sums(order):
        cells = cell[order]
        upper = (cells // low).astype(jnp.float32).astype(jnp.bfloat16)
        lower = lax.rem(cells, low).astype(jnp.float32).astype(jnp.bfloat16)
        head, tail = two_terms(frac[order] * water[order])
        zero = jnp.zeros_like(head)
        one = jnp.ones_like(head)
        picks = [upper == jnp.bfloat16(at) for at in range(high)]
        left = jnp.concatenate([jnp.where(pick, head, zero) for pick in picks] + [jnp.where(pick, tail, zero) for pick in picks], axis=0)
        right = jnp.concatenate([jnp.where(lower == jnp.bfloat16(at), one, zero) for at in range(low)], axis=0)
        both = lax.dot_general(left, right, NT, preferred_element_type=jnp.float32)
        crossed = jnp.where(same, both[: high * rows] + both[high * rows:], 0.0)
        head, tail = two_terms(crossed)
        packed = jnp.dot(jnp.concatenate([head, tail], axis=0), spread, preferred_element_type=jnp.float32)
        packed = packed[: high * rows] + packed[high * rows:]
        total = packed[:rows]
        for at in range(1, high):
            total = jnp.where(block == at, packed[at * rows:(at + 1) * rows], total)
        return total

    sends = []
    own = None
    for order, step in enumerate(steps):
        for copy in loads[order]:
            copy.wait()
        share = range(order * rows // nset, (order + 1) * rows // nset)
        for chain in share:
            matrix_loads[chain].wait()
        sums = cell_sums(order)
        for chain in share:
            head, tail = two_terms(inverse[chain].T)
            heads[chain] = head
            tails[chain] = tail
        if step == 0:
            own = sums
            continue
        part[step - 1] = sums
        if order == 0:
            pl.semaphore_wait(barrier, nset - 1 + jnp.minimum(here, 1) + jnp.minimum(npos - 1 - here, 1))
        copy = pltpu.make_async_remote_copy(
            src_ref=part.at[step - 1], dst_ref=arrived.at[step - 1],
            send_sem=part_send.at[step - 1], recv_sem=part_recv.at[step - 1],
            device_id={"tile": lax.rem(mine + step, nset)}, device_id_type=MESH)
        copy.start()
        sends.append(copy)

    for copy in small_loads:
        copy.wait()
    row = iota((rows, width), 0)
    links = jnp.zeros((rows, width), jnp.int32)
    for chain in range(rows):
        links = jnp.where(row == chain, upstream_ref[0, chain], links)
    live = mask_ref[0].astype(jnp.float32)
    rates = kappa_ref[0]
    half = rows // 2
    picked = [lax.rem(iota((2 * half, width), 0), half) == chain for chain in range(half)]

    runoff = own
    for at, copy in enumerate(sends):
        copy.wait_recv()
        runoff = runoff + arrived[at]
    forcing = time_step * runoff

    def product(vector):
        head = vector.astype(jnp.bfloat16).astype(jnp.float32)
        tail = vector - head
        starts = range(0, rows, half)
        lefts = [jnp.concatenate([head[start:start + half], tail[start:start + half]], axis=0).astype(jnp.bfloat16) for start in starts]
        totals = [jnp.zeros((2 * half, width), jnp.float32) for _ in starts]
        for chain in range(half):
            for at, start in enumerate(starts):
                single = jnp.where(picked[chain], lefts[at], jnp.zeros_like(lefts[at]))
                totals[at] += jnp.dot(single, heads[start + chain], preferred_element_type=jnp.float32)
            for at, start in enumerate(starts):
                single = jnp.where(picked[chain], lefts[at], jnp.zeros_like(lefts[at]))
                totals[at] += jnp.dot(single, tails[start + chain], preferred_element_type=jnp.float32)
        return jnp.concatenate([total[:half] + total[half:] for total in totals], axis=0)

    @pl.when(here == 0)
    def _():
        inflow[...] = jnp.zeros_like(inflow)

    level = storage_ref[0]
    outflow = level
    for substep in range(SUBSTEPS):
        copy = pltpu.make_async_remote_copy(
            src_ref=flow.at[substep], dst_ref=inflow.at[substep],
            send_sem=flow_send.at[substep], recv_sem=flow_recv.at[substep],
            device_id={"basin": lax.rem(here + 1, npos)}, device_id_type=MESH)

        @pl.when(here > 0)
        def _():
            copy.wait_recv()

        came = inflow[substep]
        incoming = jnp.broadcast_to(came[:1], (rows, width))
        for chain in range(1, rows):
            incoming = jnp.where(links == chain, jnp.broadcast_to(came[chain:chain + 1], (rows, width)), incoming)
        wet = live * product(level + forcing + incoming)
        outflow = rates * wet
        level = wet - outflow

        @pl.when(here < npos - 1)
        def _():
            flow[substep] = outflow
            copy.start()

    out_ref[0] = level
    out_ref[1] = outflow

    for copy in sends:
        copy.wait_send()

    @pl.when(here < npos - 1)
    def _():
        for substep in range(SUBSTEPS):
            pltpu.make_async_remote_copy(
                src_ref=flow.at[substep], dst_ref=inflow.at[substep],
                send_sem=flow_send.at[substep], recv_sem=flow_recv.at[substep],
                device_id={"basin": lax.rem(here + 1, npos)}, device_id_type=MESH).wait_send()


def solution(mesh):
    npos, nset = mesh.shape["basin"], mesh.shape["tile"]

    def local(tile_water, tile_frac, tile_cell, storage, kappa, inverse, cell_mask, upstream):
        rows, width = storage.shape[1:]
        tiles = tile_water.shape[2]
        anywhere = pl.BlockSpec(memory_space=pl.ANY)
        vmem = pl.BlockSpec(memory_space=pltpu.VMEM)
        out = pl.pallas_call(
            functools.partial(kernel, npos, nset),
            out_shape=jax.ShapeDtypeStruct((2, rows, width), jnp.float32),
            in_specs=[anywhere] * 8,
            out_specs=vmem,
            scratch_shapes=[
                pltpu.VMEM(storage.shape, jnp.float32),
                pltpu.VMEM(kappa.shape, jnp.float32),
                pltpu.VMEM(cell_mask.shape, jnp.int32),
                pltpu.SMEM(upstream.shape, jnp.int32),
                pltpu.VMEM((nset, rows, tiles), jnp.float32),
                pltpu.VMEM((nset, rows, tiles), jnp.float32),
                pltpu.VMEM((nset, rows, tiles), jnp.int32),
                pltpu.VMEM((rows, width, width), jnp.float32),
                pltpu.VMEM((rows, width, width), jnp.bfloat16),
                pltpu.VMEM((rows, width, width), jnp.bfloat16),
                pltpu.VMEM((nset - 1, rows, width), jnp.float32),
                pltpu.VMEM((nset - 1, rows, width), jnp.float32),
                pltpu.VMEM((SUBSTEPS, rows, width), jnp.float32),
                pltpu.VMEM((SUBSTEPS, rows, width), jnp.float32),
                pltpu.SemaphoreType.DMA((4,)),
                pltpu.SemaphoreType.DMA((nset, 3)),
                pltpu.SemaphoreType.DMA((rows,)),
                pltpu.SemaphoreType.DMA((nset - 1,)),
                pltpu.SemaphoreType.DMA((nset - 1,)),
                pltpu.SemaphoreType.DMA((SUBSTEPS,)),
                pltpu.SemaphoreType.DMA((SUBSTEPS,)),
            ],
            compiler_params=pltpu.CompilerParams(collective_id=0, has_side_effects=True),
        )(tile_water, tile_frac, tile_cell, storage, kappa, inverse, cell_mask, upstream)
        return out[:1], out[1:]

    tiled = P("basin", None, "tile")
    chain = P("basin", "tile", None)
    return jax.shard_map(
        local,
        mesh=mesh,
        in_specs=(tiled, tiled, tiled, chain, chain, P("basin", "tile", None, None), chain, P("basin", "tile")),
        out_specs=(chain, chain),
        check_vma=False,
    )
```
